256 devices in a mesh: tm: 16 (over z, y_lo), height: 16 (over x, y_hi, core).
Axes of the slice: x: 4, y: 4 (y_hi: 2, y_lo: 2; y = y_hi * 2 + y_lo), z: 8, core: 2. Of those that a mesh axis runs over, the one named last changes fastest.
Arguments:
- hidden: float32 [64, 64, 16, 1536], P('tm', 'height')
- projection: bfloat16 [1536, 4608], P('tm')
- adaptive_shift: float32 [1536], replicated, may hold values from -3 to 3
- adaptive_scale: float32 [1536], replicated, may hold values from -3 to 3
- query_gain: float32 [128], replicated, may hold values from 1 to 5.2
- key_gain: float32 [128], replicated, may hold values from 1 to 5.2
Outputs:
- attended: bfloat16 [64, 64, 16, 1536], P('tm', 'height')
The draws below stay inside these ranges and needn't reach their ends.
All inputs are finite; a program needn't handle non-finite values.
Results may differ from the reference program's by a relative error of at most 0.0075.
The reference program's roundings to bfloat16 on the way count: a program that leaves them out, or rounds other values in their place, can miss the bound.
Values may be sent and summed in bfloat16 or wider, within the bound.
No kernel may reach another device: no remote copies, remote signals or barrier semaphores. Data moves between devices by JAX's collectives and lax.ppermute only.
A program may use at most 128 MiB of HBM per device.

```python
import math
import jax
import jax.numpy as jnp
from jax import lax

D = 1536
HEADS = 12
HD = 128
TILE_T = 4
TILE_H = 4
TILE_W = 8
COLS = 16
FRAMES = 64
ROWS = 64


def draw_hidden(key, part):
    grid_shape = (FRAMES, ROWS, COLS, D)
    key_columns = jax.random.fold_in(key, 31)
    key_tokens = jax.random.fold_in(key, 32)
    key_samples = jax.random.fold_in(key, 33)
    column_scale = jnp.exp(jax.random.uniform(key_columns, (D,), jnp.float32, 0.0, math.log(10.0)))
    token_scale = jnp.exp(jax.random.uniform(key_tokens, (FRAMES, ROWS, COLS, 1), jnp.float32, 0.0, math.log(10.0)))
    samples = jax.random.truncated_normal(key_samples, -4.0, 4.0, grid_shape, jnp.float32)
    return samples * column_scale * token_scale


def draw_projection(key, part):
    inner_width = HEADS * HD
    weight_scale = D ** (-0.5)
    query_part = jax.random.truncated_normal(jax.random.fold_in(key, 41), -5.0, 5.0, (D, inner_width), jnp.float32) * weight_scale
    key_part = jax.random.truncated_normal(jax.random.fold_in(key, 42), -5.0, 5.0, (D, inner_width), jnp.float32) * weight_scale
    value_part = jax.random.truncated_normal(jax.random.fold_in(key, 43), -5.0, 5.0, (D, inner_width), jnp.float32) * weight_scale
    return jnp.concatenate([query_part, key_part, value_part], axis=1).astype(jnp.bfloat16)


def draw_query_gain(key, part):
    sub_key = jax.random.fold_in(key, 101)
    return jax.random.uniform(sub_key, (HD,), jnp.float32, 1.0, 2.0)


def draw_key_gain(key, part):
    sub_key = jax.random.fold_in(key, 202)
    return jax.random.uniform(sub_key, (HD,), jnp.float32, 1.0, 2.0)


def scatter_about(own_key, shape, width, most, held_as=jnp.bfloat16):
    values = width * jax.random.normal(own_key, shape, jnp.float32)
    return jnp.clip(values, min=-most, max=most).astype(held_as)


def setup_inputs(seed: int = 0) -> dict:
    seeds = jax.random.split(jax.random.key(seed), 7)
    hidden = draw_hidden(jax.random.fold_in(seeds[6], 71), 0)
    projection = draw_projection(jax.random.fold_in(seeds[6], 71), 0)
    adaptive_shift = scatter_about(seeds[2], (D,), 0.5, 3.0, jnp.float32)
    adaptive_scale = scatter_about(seeds[3], (D,), 0.5, 3.0, jnp.float32)
    query_gain = draw_query_gain(jax.random.fold_in(seeds[6], 71), 0)
    key_gain = draw_key_gain(jax.random.fold_in(seeds[6], 71), 0)
    return {"hidden": hidden, "projection": projection, "adaptive_shift": adaptive_shift, "adaptive_scale": adaptive_scale, "query_gain": query_gain, "key_gain": key_gain}


epsilon = 1e-06

def layer_norm(activations, adaptive_shift, adaptive_scale):
    flattened = activations.reshape(-1, activations.shape[-1])
    centre = lax.optimization_barrier(jnp.mean(flattened, axis=1, keepdims=True))
    shifted = flattened - centre
    spread = lax.optimization_barrier(jnp.mean(shifted * shifted, axis=1, keepdims=True))
    scaled = shifted * lax.rsqrt(spread + epsilon) * (1.0 + adaptive_scale) + adaptive_shift
    return scaled.astype(jnp.bfloat16)

def head_norm(activations, head_gain):
    by_head = activations.reshape(activations.shape[0], -1, head_gain.shape[0])
    mean_square = lax.optimization_barrier(jnp.mean(by_head * by_head, axis=2, keepdims=True))
    return (by_head * lax.rsqrt(mean_square + epsilon) * head_gain).reshape(activations.shape).astype(jnp.bfloat16)

def reference(hidden, projection, adaptive_shift, adaptive_scale, query_gain, key_gain):
    inner_width = HEADS * HD
    tile_tokens = TILE_T * TILE_H * TILE_W
    time_tiles = FRAMES // TILE_T
    row_tiles = ROWS // TILE_H
    width_tiles = COLS // TILE_W
    weight_wide = projection.astype(jnp.float32)

    def project_frame(frame_rows):
        normed = layer_norm(frame_rows, adaptive_shift, adaptive_scale)
        projected = jnp.dot(normed.astype(jnp.float32), weight_wide, preferred_element_type=jnp.float32)
        queries = head_norm(projected[:, :inner_width], query_gain)
        keys = head_norm(projected[:, inner_width:2 * inner_width], key_gain)
        values = projected[:, 2 * inner_width:].astype(jnp.bfloat16)
        return (queries, keys, values)
    queries, keys, values = lax.map(project_frame, hidden)

    def to_tiles(tensor_grid):
        pieces = tensor_grid.reshape(time_tiles, TILE_T, row_tiles, TILE_H, width_tiles, TILE_W, inner_width)
        return pieces.transpose(0, 2, 4, 1, 3, 5, 6).reshape(time_tiles, row_tiles, width_tiles, tile_tokens, inner_width)
    width_pad = 1 if width_tiles > 1 else 0
    window_width = 3 if width_tiles > 1 else 1
    padding = ((1, 1), (1, 1), (width_pad, width_pad), (0, 0), (0, 0))
    key_tiles = jnp.pad(to_tiles(keys), padding)
    value_tiles = jnp.pad(to_tiles(values), padding)
    query_tiles = to_tiles(queries).reshape(-1, tile_tokens, inner_width)
    offsets = jnp.arange(3, dtype=jnp.int32) - 1
    score_scale = HD ** (-0.5)
    zero_index = jnp.zeros((), jnp.int32)

    def attend(tile_number):
        time_index = tile_number // (row_tiles * width_tiles)
        row_index = tile_number // width_tiles % row_tiles
        width_index = tile_number % width_tiles
        window_start = (time_index, row_index, width_index, zero_index, zero_index)
        window_size = (3, 3, window_width, tile_tokens, inner_width)
        key_window = lax.dynamic_slice(key_tiles, window_start, window_size).reshape(-1, HEADS, HD).astype(jnp.float32)
        value_window = lax.dynamic_slice(value_tiles, window_start, window_size).reshape(-1, HEADS, HD).astype(jnp.float32)
        time_ok = (time_index + offsets >= 0) & (time_index + offsets < time_tiles)
        row_ok = (row_index + offsets >= 0) & (row_index + offsets < row_tiles)
        if width_tiles > 1:
            width_ok = (width_index + offsets >= 0) & (width_index + offsets < width_tiles)
        else:
            width_ok = jnp.ones((1,), dtype=bool)
        tile_ok = time_ok[:, None, None] & row_ok[None, :, None] & width_ok[None, None, :]
        key_ok = jnp.broadcast_to(tile_ok[:, :, :, None], (3, 3, window_width, tile_tokens)).reshape(-1)
        query_rows = lax.dynamic_index_in_dim(query_tiles, tile_number, 0, keepdims=False)
        query_rows = query_rows.reshape(tile_tokens, HEADS, HD).astype(jnp.float32)
        scores = jnp.einsum('shd,khd->hsk', query_rows, key_window) * score_scale
        scores = jnp.where(key_ok[None, None, :], scores, -jnp.inf)
        row_peak = lax.optimization_barrier(jnp.max(scores, axis=2, keepdims=True))
        weights = jnp.exp(scores - row_peak)
        totals = lax.optimization_barrier(jnp.sum(weights, axis=2, keepdims=True))
        rounded = lax.optimization_barrier(weights.astype(jnp.bfloat16)).astype(jnp.float32)
        mixture = jnp.einsum('hsk,khd->hsd', rounded, value_window) / totals
        return mixture.transpose(1, 0, 2).reshape(tile_tokens, inner_width).astype(jnp.bfloat16)
    attended = lax.map(attend, jnp.arange(time_tiles * row_tiles * width_tiles, dtype=jnp.int32))
    attended = attended.reshape(time_tiles, row_tiles, width_tiles, TILE_T, TILE_H, TILE_W, inner_width)
    return attended.transpose(0, 3, 1, 4, 2, 5, 6).reshape(FRAMES, ROWS, COLS, inner_width)
```

```python
import math

import jax
import jax.numpy as jnp
import numpy as np
from jax import lax
from jax.experimental import pallas as pl
from jax.experimental.pallas import tpu as pltpu
from jax.sharding import Mesh, PartitionSpec as P

AXES = ("z", "yl", "x", "yh", "core")
SIZES = (8, 2, 4, 2, 2)
TOKENS = 256
D = 1536
HD = 128
GROUP_HEADS = 3
GROUP = GROUP_HEADS * HD
ROWS = 96
EPSILON = 1e-06
SCORE_SCALE = HD ** (-0.5) * math.log2(math.e)
F32 = jnp.float32
BF16 = jnp.bfloat16


def linear(z, y, x, core):
    return (((z % 8 * 2 + y % 2) * 4 + x % 4) * 2 + y % 4 // 2) * 2 + core


def pairs(move):
    return [
        (linear(z, y, x, core), linear(*move(z, y, x, core)))
        for z in range(8)
        for y in range(4)
        for x in range(4)
        for core in range(2)
    ]


def shift(array, dz=0, dy=0):
    return lax.ppermute(array, AXES, pairs(lambda z, y, x, core: (z + dz, y + dy, x, core)))


def swap_cores(array):
    return lax.ppermute(array, AXES, pairs(lambda z, y, x, core: (z, y, x, 1 - core)))


def outward(array, dz=0):
    return lax.ppermute(
        array, AXES, pairs(lambda z, y, x, core: (z + dz, y, x + (1 if core else -1), 1 - core))
    )


def swap_rows_owner(array):
    def move(z, y, x, core):
        yh, yl = y // 2, y % 2
        return (z, y, x, core) if core == yl else (z, yh * 2 + 1 - yl, x, 1 - core)

    return lax.ppermute(array, AXES, pairs(move))


def layer_norm(activations, adaptive_shift, adaptive_scale):
    centre = jnp.mean(activations, axis=1, keepdims=True)
    shifted = activations - centre
    spread = jnp.mean(shifted * shifted, axis=1, keepdims=True)
    scaled = shifted * lax.rsqrt(spread + EPSILON) * (1.0 + adaptive_scale) + adaptive_shift
    return scaled.astype(BF16)


STEPS = (0, 1, -1, 2)
HOPS = (0, 4, 3, -3, 2, -2, 1, -1)


def project_kernel(place, *refs):
    tokens = refs[:4]
    mine, other, query_gain, key_gain = refs[4:8]
    q_out, own, low, high, edge, edge_low, edge_high = refs[8:15]
    weights = refs[15]
    z, y, core = place[0], place[1], place[2]
    for index, hop in enumerate(HOPS):
        start = lax.rem(z - hop + 8, 8) * (2 * ROWS)
        weights[pl.ds(pl.multiple_of(start + core * ROWS, 32), ROWS), :] = mine[index]
        weights[pl.ds(pl.multiple_of(start + (1 - core) * ROWS, 32), ROWS), :] = other[index]

    def head_norm(block, gain):
        mean_square = jnp.mean(block * block, axis=1, keepdims=True)
        return (block * lax.rsqrt(mean_square + EPSILON) * gain[...]).astype(BF16)

    for index, step in enumerate(STEPS):
        source = lax.rem(y - step + 4, 4)
        yl = lax.rem(source, 2)
        role = jnp.where(source // 2 == core, 0, 1)
        rows = tokens[index][...]
        projected = jnp.dot(rows, weights[...], preferred_element_type=F32)
        for head in range(GROUP_HEADS):
            part = lambda kind: projected[:, kind * GROUP + head * HD : kind * GROUP + (head + 1) * HD]
            q = head_norm(part(0), query_gain)
            k = head_norm(part(1), key_gain)
            v = part(2).astype(BF16)
            q_out[yl * 2 + role, :, head * HD : (head + 1) * HD] = q
            ks = slice(head * 2 * HD, head * 2 * HD + HD)
            vs = slice(head * 2 * HD + HD, (head + 1) * 2 * HD)
            own[yl, role, :, ks] = k
            own[yl, role, :, vs] = v
    low[...] = own[0]
    high[...] = own[1]
    edge[...] = own[:, 0]
    edge_low[...] = own[0, 0]
    edge_high[...] = own[1, 0]


def project(place, tokens, mine, other, query_gain, key_gain):
    vmem = pl.BlockSpec(memory_space=pltpu.VMEM)
    kv = lambda *lead: jax.ShapeDtypeStruct(lead + (TOKENS, 2 * GROUP), BF16)
    return pl.pallas_call(
        project_kernel,
        name="project",
        out_shape=(
            jax.ShapeDtypeStruct((4, TOKENS, GROUP), BF16),
            kv(2, 2),
            kv(2),
            kv(2),
            kv(2),
            kv(),
            kv(),
        ),
        in_specs=[pl.BlockSpec(memory_space=pltpu.SMEM)] + [vmem] * 8,
        out_specs=[vmem] * 7,
        scratch_shapes=[pltpu.VMEM((D, 3 * GROUP), BF16)],
        compiler_params=pltpu.CompilerParams(vmem_limit_bytes=48 * 1024 * 1024),
        cost_estimate=pl.CostEstimate(
            flops=2 * 4 * TOKENS * D * 3 * GROUP, bytes_accessed=12_000_000, transcendentals=0
        ),
    )(place, *tokens, mine, other, query_gain.reshape(1, HD), key_gain.reshape(1, HD))


def attend_kernel(valid, q, own, mate, below, above, mate_below, mate_above, edge, edge_below, edge_above, out):
    penalty = lambda flag: jnp.where(flag > 0, 0.0, 1e30).astype(F32)
    no_below = penalty(valid[0])
    no_above = penalty(valid[1])
    no_edge = penalty(valid[2])
    core = valid[3]
    ones = jnp.ones((TOKENS, HD), BF16)
    for yl in range(2):
        row, mate_row, edge_row, no_row = (
            (below, mate_below, edge_below, no_below) if yl == 0 else (above, mate_above, edge_above, no_above)
        )
        for role in range(2):
            if role == 0:
                groups = [
                    (None, [own[0, 0], own[1, 0], mate[0, 1], mate[1, 1]]),
                    (no_row, [row[0], mate_row[1]]),
                    (no_edge, [edge[0], edge[1]]),
                    (jnp.maximum(no_row, no_edge), [edge_row[...]]),
                ]
            else:
                groups = [
                    (None, [own[0, 1], own[1, 1], mate[0, 0], mate[1, 0], mate[0, 1], mate[1, 1]]),
                    (no_row, [row[1], mate_row[0], mate_row[1]]),
                ]
            query = q[yl * 2 + role]
            scored = []
            peak = None
            for cost, tiles in groups:
                top = None
                for tile in tiles:
                    scores = lax.dot_general(
                        query, tile[:, :HD], (((1,), (1,)), ((), ())), preferred_element_type=F32
                    )
                    scored.append((cost, tile, scores))
                    top = scores if top is None else jnp.maximum(top, scores)
                top = jnp.max(top, axis=1, keepdims=True)
                if cost is not None:
                    top = top - cost
                peak = top if peak is None else jnp.maximum(peak, top)
            peak = peak * SCORE_SCALE
            total = None
            for cost, tile, scores in scored:
                base = peak if cost is None else peak + cost
                weights = jnp.exp2(scores * SCORE_SCALE - base).astype(BF16)
                wide = jnp.concatenate([tile[:, HD:], ones], axis=1)
                mixed = jnp.dot(weights, wide, preferred_element_type=F32)
                total = mixed if total is None else total + mixed
            yh = core if role == 0 else 1 - core
            out[yh * 2 + yl] = (total[:, :HD] / total[:, HD:]).astype(BF16)


def attend(valid, q, *kv):
    def spec(array, width):
        lead = array.ndim - 1
        return pl.BlockSpec(array.shape[:-1] + (width,), lambda h: (0,) * lead + (h,))

    return pl.pallas_call(
        attend_kernel,
        name="attend",
        grid=(GROUP_HEADS,),
        out_shape=jax.ShapeDtypeStruct((4, TOKENS, GROUP), BF16),
        in_specs=[pl.BlockSpec(memory_space=pltpu.SMEM), spec(q, HD)] + [spec(a, 2 * HD) for a in kv],
        out_specs=pl.BlockSpec((4, TOKENS, HD), lambda h: (0, 0, h)),
        compiler_params=pltpu.CompilerParams(
            dimension_semantics=("arbitrary",), vmem_limit_bytes=48 * 1024 * 1024
        ),
        cost_estimate=pl.CostEstimate(
            flops=4 * 12 * TOKENS * 9 * TOKENS * HD,
            bytes_accessed=10_000_000,
            transcendentals=12 * TOKENS * 9 * TOKENS,
        ),
    )(valid, q, *kv)


def per_device(hidden, projection, adaptive_shift, adaptive_scale, query_gain, key_gain):
    z, yl, x, yh, core = (lax.axis_index(a) for a in AXES)
    y = yh * 2 + yl

    inner = projection.shape[1] // 3
    start = (yh * 2 + core) * GROUP
    columns = jnp.concatenate(
        [lax.dynamic_slice_in_dim(projection, kind * inner + start, GROUP, 1) for kind in range(3)], axis=1
    )
    base = swap_rows_owner(columns)
    mine = jnp.stack([base] + [shift(base, dz=hop) for hop in HOPS[1:]])
    other = swap_cores(mine)

    normed = layer_norm(hidden.reshape(TOKENS, D), adaptive_shift, adaptive_scale)
    tokens = [normed] + [shift(normed, dy=step) for step in STEPS[1:]]

    place = jnp.stack([z, y, core]).astype(jnp.int32)
    q, own, low, high, edge, edge_low, edge_high = project(place, tokens, mine, other, query_gain, key_gain)
    mate = swap_cores(own)
    below = shift(high, dz=1)
    above = shift(low, dz=-1)
    edge_in = outward(edge)
    edge_below = outward(edge_high, dz=1)
    edge_above = outward(edge_low, dz=-1)
    mate_below = swap_cores(below)
    mate_above = swap_cores(above)
    last_x = jnp.where(core == 0, 0, 3)
    valid = jnp.stack([z > 0, z < 7, x != last_x, core]).astype(jnp.int32)
    attended = attend(
        valid, q, own, mate, below, above, mate_below, mate_above, edge_in, edge_below, edge_above
    )
    back = lax.all_to_all(attended, ("yh", "yl"), 0, 0)
    return jnp.transpose(back, (1, 0, 2)).reshape(hidden.shape)


def solution(mesh):
    split = Mesh(np.asarray(mesh.devices).reshape(SIZES), AXES)
    tm, height = ("z", "yl"), ("x", "yh", "core")
    return jax.shard_map(
        per_device,
        mesh=split,
        in_specs=(P(tm, height, None, None), P(tm, None), P(), P(), P(), P()),
        out_specs=P(tm, height, None, None),
        check_vma=False,
    )
```

```python
import math

import jax
import jax.numpy as jnp
import numpy as np
from jax import lax
from jax.experimental import pallas as pl
from jax.experimental.pallas import tpu as pltpu
from jax.sharding import Mesh, PartitionSpec as P

AXES = ("z", "yl", "x", "yh", "core")
SIZES = (8, 2, 4, 2, 2)
TOKENS = 256
D = 1536
HD = 128
GROUP_HEADS = 3
GROUP = GROUP_HEADS * HD
ROWS = 96
EPSILON = 1e-06
SCORE_SCALE = HD ** (-0.5) * math.log2(math.e)
F32 = jnp.float32
BF16 = jnp.bfloat16


def linear(z, y, x, core):
    return (((z % 8 * 2 + y % 2) * 4 + x % 4) * 2 + y % 4 // 2) * 2 + core


def pairs(move):
    return [
        (linear(z, y, x, core), linear(*move(z, y, x, core)))
        for z in range(8)
        for y in range(4)
        for x in range(4)
        for core in range(2)
    ]


def shift(array, dz=0, dy=0):
    return lax.ppermute(array, AXES, pairs(lambda z, y, x, core: (z + dz, y + dy, x, core)))


def swap_cores(array):
    return lax.ppermute(array, AXES, pairs(lambda z, y, x, core: (z, y, x, 1 - core)))


def outward(array, dz=0):
    return lax.ppermute(
        array, AXES, pairs(lambda z, y, x, core: (z + dz, y, x + (1 if core else -1), 1 - core))
    )


def ring_step(array):
    return lax.ppermute(
        array, AXES, pairs(lambda z, y, x, core: (z + (-1 if core else 1), y, x, core))
    )


def swap_rows(array):
    return lax.ppermute(
        array, AXES, pairs(lambda z, y, x, core: (z, y // 2 * 2 + 1 - y % 2, x, core))
    )


def after(array, *others):
    return lax.optimization_barrier((array,) + others)[0]


def layer_norm(activations, adaptive_shift, adaptive_scale):
    centre = jnp.mean(activations, axis=1, keepdims=True)
    shifted = activations - centre
    spread = jnp.mean(shifted * shifted, axis=1, keepdims=True)
    scaled = shifted * lax.rsqrt(spread + EPSILON) * (1.0 + adaptive_scale) + adaptive_shift
    return scaled.astype(BF16)


STEPS = (0, 1, -1, 2)
HALF = TOKENS // 2
VMEM = pl.BlockSpec(memory_space=pltpu.VMEM)
SMEM = pl.BlockSpec(memory_space=pltpu.SMEM)
PARAMS = pltpu.CompilerParams(vmem_limit_bytes=60 * 1024 * 1024)
WIDE = pltpu.CompilerParams(vmem_limit_bytes=16 * 1024 * 1024)


def weight_copies(weights, pieces, sems, z, yl, core):
    sign = 2 * core - 1
    offsets = [0] + [sign * r for r in range(1, 5)] + [-sign * r for r in range(1, 4)]
    copies = []
    for index, (piece, offset) in enumerate(zip(pieces, offsets, strict=True)):
        start = lax.rem(z + offset + 8, 8) * (2 * ROWS)
        for half, lo in ((0, yl), (1, 1 - yl)):
            where = pl.ds(pl.multiple_of(start + lo * ROWS, 32), ROWS)
            copies.append(
                pltpu.make_async_copy(
                    piece.at[pl.ds(half * ROWS, ROWS)], weights.at[where], sems.at[2 * index + half]
                )
            )
    return copies


def head_norm(block, gain):
    mean_square = jnp.mean(block * block, axis=1, keepdims=True)
    return (block * lax.rsqrt(mean_square + EPSILON) * gain[...]).astype(BF16)


def sources(y, core):
    found = []
    for step in STEPS:
        source = lax.rem(y - step + 4, 4)
        found.append((lax.rem(source, 2), jnp.where(source // 2 == core, 0, 1)))
    return found


def token_copies(rows, tokens, slots, sems):
    copies = [pltpu.make_async_copy(tokens[n], rows.at[slots[n]], sems.at[n]) for n in range(3)]
    for half in range(2):
        where = rows.at[slots[3], pl.ds(half * HALF, HALF)]
        copies.append(pltpu.make_async_copy(tokens[3 + half], where, sems.at[3 + half]))
    return copies


def project_kernel(place, *refs):
    tokens, pieces = refs[:5], refs[5:13]
    query_gain, key_gain, q_out, own, edge = refs[13:18]
    alone = refs[18:22]
    weights, rows, sems, token_sems = refs[22:]
    y, core = place[0], place[1]
    slots = [role * 2 + yl for yl, role in sources(y, core)]
    copies = weight_copies(weights, pieces, sems, place[2], lax.rem(y, 2), core)
    copies += token_copies(rows, tokens, slots, token_sems)
    for copy in copies:
        copy.start()
    for copy in copies:
        copy.wait()
    for slot in range(4):
        role, yl = slot // 2, slot % 2
        projected = jnp.dot(rows[slot], weights[...], preferred_element_type=F32)
        for head in range(GROUP_HEADS):
            ks = slice(head * 2 * HD, head * 2 * HD + HD)
            vs = slice(head * 2 * HD + HD, (head + 1) * 2 * HD)
            span = slice(head * HD, (head + 1) * HD)
            part = lambda kind: projected[:, kind * GROUP + head * HD : kind * GROUP + (head + 1) * HD]
            k = head_norm(part(0), key_gain)
            v = part(1).astype(BF16)
            for out in [own.at[role, yl], alone[slot]] + ([edge.at[yl]] if role == 0 else []):
                out[:, ks] = k
                out[:, vs] = v
            q_out[slot, :, span] = head_norm(part(2), query_gain)


ANY = pl.BlockSpec(memory_space=pl.ANY)
LIGHT = pl.CostEstimate(flops=10_000_000, bytes_accessed=100_000, transcendentals=0)


def project(place, tokens, pieces, query_gain, key_gain):
    kv = lambda *lead: jax.ShapeDtypeStruct(lead + (TOKENS, 2 * GROUP), BF16)
    return pl.pallas_call(
        project_kernel,
        name="project",
        out_shape=(jax.ShapeDtypeStruct((4, TOKENS, GROUP), BF16), kv(2, 2), kv(2)) + (kv(),) * 4,
        in_specs=[SMEM] + [ANY] * 13 + [VMEM] * 2,
        out_specs=[VMEM] * 7,
        scratch_shapes=[
            pltpu.VMEM((D, 3 * GROUP), BF16),
            pltpu.VMEM((4, TOKENS, D), BF16),
            pltpu.SemaphoreType.DMA((16,)),
            pltpu.SemaphoreType.DMA((5,)),
        ],
        compiler_params=PARAMS,
        cost_estimate=LIGHT,
    )(place, *tokens, *pieces, query_gain.reshape(1, HD), key_gain.reshape(1, HD))


def fold(scores):
    return jnp.maximum(scores[:, :HD], scores[:, HD:])


def attend_tiles(query, groups, peak, total):
    ones = jnp.ones((TOKENS, HD), BF16)
    scored = []
    best = peak
    for cost, tiles in groups:
        top = None
        for tile in tiles:
            scores = lax.dot_general(
                query, tile[:, :HD], (((1,), (1,)), ((), ())), preferred_element_type=F32
            )
            scored.append((cost, scores))
            folded = fold(scores)
            top = folded if top is None else jnp.maximum(top, folded)
        top = top * SCORE_SCALE
        if cost is not None:
            top = top - cost
        best = top if best is None else jnp.maximum(best, top)
    high = jnp.max(best, axis=1, keepdims=True)
    weights = []
    for cost, scores in scored:
        base = high if cost is None else high + cost
        weights.append(jnp.exp2(scores * SCORE_SCALE - base).astype(BF16))
    wide = [jnp.concatenate([tile[:, HD:], ones], axis=1) for _, tiles in groups for tile in tiles]
    mixed = jnp.dot(
        jnp.concatenate(weights, axis=1), jnp.concatenate(wide, axis=0), preferred_element_type=F32
    )
    if total is not None:
        scale = jnp.exp2(peak - high)
        mixed = mixed + total * jnp.concatenate([scale, scale], axis=1)
    return high, mixed


def penalty(flag):
    return jnp.where(flag > 0, 0.0, 1e30).astype(F32)


def near_kernel(valid, q, own, mate, edge, below, above, peaks, totals):
    no_edge = penalty(valid[2])
    for yl in range(2):
        no_row, row = (penalty(valid[1]), above) if yl else (penalty(valid[0]), below)
        for role in range(2):
            slot = role * 2 + yl
            if role == 0:
                groups = [
                    (None, [own[0, 0], own[0, 1], mate[1, 0], mate[1, 1]]),
                    (no_edge, [edge[0], edge[1]]),
                    (no_row, [row[...]]),
                ]
            else:
                groups = [
                    (None, [own[1, 0], own[1, 1], mate[1, 0], mate[1, 1], mate[0, 0], mate[0, 1]])
                ]
            peak, total = attend_tiles(q[slot], groups, None, None)
            peaks[0, slot] = jnp.broadcast_to(peak, (TOKENS, HD))
            totals[0, slot] = total


def far_kernel(valid, q, peaks, totals, *refs):
    inner_rows, mate_outer_rows, mate_inner_rows, corners = refs[0:2], refs[2:4], refs[4:6], refs[6:8]
    outs, done = refs[8:12], refs[12]
    core = valid[3]
    for yl in range(2):
        no_row = penalty(valid[yl])
        for role in range(2):
            slot = role * 2 + yl
            if role == 0:
                groups = [
                    (no_row, [mate_inner_rows[yl][...]]),
                    (jnp.maximum(no_row, penalty(valid[2])), [corners[yl][...]]),
                ]
            else:
                groups = [(no_row, [rows[yl][...] for rows in (inner_rows, mate_inner_rows, mate_outer_rows)])]
            _, total = attend_tiles(q[slot], groups, peaks[0, slot], totals[0, slot])
            yh = 1 - core if role else core
            done[yh * 2 + yl] = (total[:, :HD] / total[:, HD:]).astype(BF16)
    for out, step in zip(outs, STEPS, strict=True):
        out[...] = done[lax.rem(valid[4] - step + 4, 4)]


def head_spec(array, width):
    lead = array.ndim - 1
    return pl.BlockSpec(array.shape[:-1] + (width,), lambda h: (0,) * lead + (h,))


STATE = lambda width: pl.BlockSpec((1, 4, TOKENS, width), lambda h: (h, 0, 0, 0))


def attend_near(valid, q, *kv):
    return pl.pallas_call(
        near_kernel,
        name="attend_near",
        grid=(GROUP_HEADS,),
        out_shape=(
            jax.ShapeDtypeStruct((GROUP_HEADS, 4, TOKENS, HD), F32),
            jax.ShapeDtypeStruct((GROUP_HEADS, 4, TOKENS, 2 * HD), F32),
        ),
        in_specs=[SMEM, head_spec(q, HD)] + [head_spec(a, 2 * HD) for a in kv],
        out_specs=[STATE(HD), STATE(2 * HD)],
        compiler_params=WIDE,
        cost_estimate=LIGHT,
    )(valid, q, *kv)


def attend_far(valid, q, peaks, totals, *kv):
    return pl.pallas_call(
        far_kernel,
        name="attend_far",
        grid=(GROUP_HEADS,),
        out_shape=(jax.ShapeDtypeStruct((TOKENS, GROUP), BF16),) * 4,
        in_specs=[SMEM, head_spec(q, HD), STATE(HD), STATE(2 * HD)] + [head_spec(a, 2 * HD) for a in kv],
        out_specs=[pl.BlockSpec((TOKENS, HD), lambda h: (0, h))] * 4,
        scratch_shapes=[pltpu.VMEM((4, TOKENS, HD), BF16)],
        compiler_params=WIDE,
        cost_estimate=LIGHT,
    )(valid, q, peaks, totals, *kv)


def side_kernel(place, *refs):
    for part, step in zip(refs[:4], STEPS, strict=True):
        start = lax.rem(place[0] + step + 4, 4) * GROUP
        refs[4][:, pl.ds(pl.multiple_of(start, HD), GROUP)] = part[...]


def side_by_side(place, parts, shape):
    return pl.pallas_call(
        side_kernel,
        name="side_by_side",
        out_shape=jax.ShapeDtypeStruct((TOKENS, D), BF16),
        in_specs=[SMEM] + [VMEM] * 4,
        out_specs=VMEM,
        compiler_params=WIDE,
    )(place, *parts).reshape(shape)


def per_device(hidden, projection, adaptive_shift, adaptive_scale, query_gain, key_gain):
    z, yl, x, yh, core = (lax.axis_index(a) for a in AXES)
    y = yh * 2 + yl
    inner = projection.shape[1] // 3

    def columns(chip, *kinds):
        parts = [lax.dynamic_slice_in_dim(projection, k * inner + chip * GROUP, GROUP, 1) for k in kinds]
        return parts[0] if len(parts) == 1 else jnp.concatenate(parts, axis=1)

    normed = layer_norm(hidden.reshape(TOKENS, D), adaptive_shift, adaptive_scale)
    theirs = swap_rows(columns(yh * 2 + 1 - yl, 1, 2, 0))
    normed = after(normed, theirs)
    behind, ahead = shift(normed, dy=1), shift(normed, dy=-1)
    base = jnp.concatenate([columns(y, 1, 2, 0), theirs], axis=0)
    base = after(base, normed)
    ring = [base, ring_step(base)]
    ring.append(ring_step(ring[1]))
    ring.append(ring_step(after(ring[2], behind, ahead)))
    ring.append(ring_step(ring[3]))
    pieces = ring + [swap_cores(piece) for piece in ring[1:4]]
    tokens = [normed, behind, ahead, shift(behind[:HALF], dy=1), shift(ahead[HALF:], dy=-1)]

    place = jnp.stack([y, core, z]).astype(jnp.int32)
    q, own, edge_out, outer_low, outer_high, inner_low, inner_high = project(
        place, tokens, pieces, query_gain, key_gain
    )
    outer_below = shift(outer_high, dz=1)
    outer_above = shift(outer_low, dz=-1)
    edge = outward(edge_out)
    mate = swap_cores(own)
    inner_below = shift(after(inner_high, mate), dz=1)
    inner_above = shift(after(inner_low, mate), dz=-1)
    corner_below = outward(outer_below)
    corner_above = outward(outer_above)
    last_x = jnp.where(core == 0, 0, 3)
    valid = jnp.stack([z > 0, z < 7, x != last_x, core, y]).astype(jnp.int32)
    peaks, totals = attend_near(valid, q, own, mate, edge, outer_below, outer_above)
    mate_outer_rows = [swap_cores(after(row, peaks)) for row in (outer_below, outer_above)]
    inner_rows = [inner_below, inner_above]
    mate_inner_rows = [swap_cores(after(row, peaks)) for row in inner_rows]
    attended = attend_far(
        valid, q, peaks, totals, *inner_rows, *mate_outer_rows, *mate_inner_rows, corner_below, corner_above
    )
    back = [attended[0]] + [shift(tile, dy=-step) for step, tile in zip(STEPS[1:], attended[1:], strict=True)]
    return side_by_side(place, back, hidden.shape)


def solution(mesh):
    split = Mesh(np.asarray(mesh.devices).reshape(SIZES), AXES)
    tm, height = ("z", "yl"), ("x", "yh", "core")
    return jax.shard_map(
        per_device,
        mesh=split,
        in_specs=(P(tm, height, None, None), P(tm, None), P(), P(), P(), P()),
        out_specs=P(tm, height, None, None),
        check_vma=False,
    )
```

```python
import math

import jax
import jax.numpy as jnp
import numpy as np
from jax import lax
from jax.experimental import pallas as pl
from jax.experimental.pallas import tpu as pltpu
from jax.sharding import Mesh, PartitionSpec as P

AXES = ("z", "yl", "x", "yh", "core")
SIZES = (8, 2, 4, 2, 2)
TOKENS = 256
D = 1536
HD = 128
GROUP_HEADS = 3
GROUP = GROUP_HEADS * HD
ROWS = 96
EPSILON = 1e-06
SCORE_SCALE = HD ** (-0.5) * math.log2(math.e)
F32 = jnp.float32
BF16 = jnp.bfloat16


def linear(z, y, x, core):
    return (((z % 8 * 2 + y % 2) * 4 + x % 4) * 2 + y % 4 // 2) * 2 + core


def pairs(move):
    return [
        (linear(z, y, x, core), linear(*move(z, y, x, core)))
        for z in range(8)
        for y in range(4)
        for x in range(4)
        for core in range(2)
    ]


def shift(array, dz=0, dy=0):
    return lax.ppermute(array, AXES, pairs(lambda z, y, x, core: (z + dz, y + dy, x, core)))


def swap_cores(array):
    return lax.ppermute(array, AXES, pairs(lambda z, y, x, core: (z, y, x, 1 - core)))


def outward(array, dz=0):
    return lax.ppermute(
        array, AXES, pairs(lambda z, y, x, core: (z + dz, y, x + (1 if core else -1), 1 - core))
    )


def ring_step(array):
    return lax.ppermute(
        array, AXES, pairs(lambda z, y, x, core: (z + (-1 if core else 1), y, x, core))
    )


def swap_rows(array):
    return lax.ppermute(
        array, AXES, pairs(lambda z, y, x, core: (z, y // 2 * 2 + 1 - y % 2, x, core))
    )


def after(array, *others):
    return lax.optimization_barrier((array,) + others)[0]


def layer_norm(activations, adaptive_shift, adaptive_scale):
    centre = jnp.mean(activations, axis=1, keepdims=True)
    shifted = activations - centre
    spread = jnp.mean(shifted * shifted, axis=1, keepdims=True)
    scaled = shifted * lax.rsqrt(spread + EPSILON) * (1.0 + adaptive_scale) + adaptive_shift
    return scaled.astype(BF16)


STEPS = (0, 1, -1, 2)
HALF = TOKENS // 2
VMEM = pl.BlockSpec(memory_space=pltpu.VMEM)
SMEM = pl.BlockSpec(memory_space=pltpu.SMEM)
PARAMS = pltpu.CompilerParams(vmem_limit_bytes=60 * 1024 * 1024)
NEAR = pltpu.CompilerParams(vmem_limit_bytes=60 * 1024 * 1024)
FAR = pltpu.CompilerParams(vmem_limit_bytes=60 * 1024 * 1024)
SIDE = pltpu.CompilerParams(vmem_limit_bytes=8 * 1024 * 1024)


def weight_copies(weights, pieces, sems, z, yl, core):
    sign = 2 * core - 1
    offsets = [0] + [sign * r for r in range(1, 5)] + [-sign * r for r in range(1, 4)]
    copies = []
    for index, (piece, offset) in enumerate(zip(pieces, offsets, strict=True)):
        start = lax.rem(z + offset + 8, 8) * (2 * ROWS)
        for half, lo in ((0, yl), (1, 1 - yl)):
            where = pl.ds(pl.multiple_of(start + lo * ROWS, 32), ROWS)
            copies.append(
                pltpu.make_async_copy(
                    piece.at[pl.ds(half * ROWS, ROWS)], weights.at[where], sems.at[2 * index + half]
                )
            )
    return copies


def head_norm(block, gain):
    mean_square = jnp.mean(block * block, axis=1, keepdims=True)
    return (block * lax.rsqrt(mean_square + EPSILON) * gain[...]).astype(BF16)


def sources(y, core):
    found = []
    for step in STEPS:
        source = lax.rem(y - step + 4, 4)
        found.append((lax.rem(source, 2), jnp.where(source // 2 == core, 0, 1)))
    return found


def token_copies(rows, tokens, slots, sems):
    copies = [pltpu.make_async_copy(tokens[n], rows.at[slots[n]], sems.at[n]) for n in range(3)]
    for half in range(2):
        where = rows.at[slots[3], pl.ds(half * HALF, HALF)]
        copies.append(pltpu.make_async_copy(tokens[3 + half], where, sems.at[3 + half]))
    return copies


def project_kernel(place, *refs):
    tokens, pieces = refs[:5], refs[5:13]
    query_gain, key_gain, q_out, own, edge = refs[13:18]
    alone = refs[18:22]
    weights, rows, q_done, kv_done, sems, token_sems, out_sems = refs[22:]
    y, core = place[0], place[1]
    slots = [role * 2 + yl for yl, role in sources(y, core)]
    copies = weight_copies(weights, pieces, sems, place[2], lax.rem(y, 2), core)
    copies += token_copies(rows, tokens, slots, token_sems)
    for copy in copies:
        copy.start()
    for copy in copies:
        copy.wait()
    leaving = []
    for slot in range(4):
        role, yl = slot // 2, slot % 2
        projected = jnp.dot(rows[slot], weights[...], preferred_element_type=F32)
        for head in range(GROUP_HEADS):
            ks = slice(head * 2 * HD, head * 2 * HD + HD)
            vs = slice(head * 2 * HD + HD, (head + 1) * 2 * HD)
            span = slice(head * HD, (head + 1) * HD)
            part = lambda kind: projected[:, kind * GROUP + head * HD : kind * GROUP + (head + 1) * HD]
            kv_done[slot, :, ks] = head_norm(part(0), key_gain)
            kv_done[slot, :, vs] = part(1).astype(BF16)
            q_done[slot, :, span] = head_norm(part(2), query_gain)
        targets = [own.at[role, yl], alone[slot]] + ([edge.at[yl]] if role == 0 else [])
        moves = [(kv_done.at[slot], target) for target in targets] + [(q_done.at[slot], q_out.at[slot])]
        for index, (source, target) in enumerate(moves):
            leaving.append(pltpu.make_async_copy(source, target, out_sems.at[slot, index]))
            leaving[-1].start()
    for copy in leaving:
        copy.wait()


ANY = pl.BlockSpec(memory_space=pl.ANY)
LIGHT = pl.CostEstimate(flops=10_000_000, bytes_accessed=100_000, transcendentals=0)


def project(place, tokens, pieces, query_gain, key_gain):
    kv = lambda *lead: jax.ShapeDtypeStruct(lead + (TOKENS, 2 * GROUP), BF16)
    return pl.pallas_call(
        project_kernel,
        name="project",
        out_shape=(jax.ShapeDtypeStruct((4, TOKENS, GROUP), BF16), kv(2, 2), kv(2)) + (kv(),) * 4,
        in_specs=[SMEM] + [ANY] * 13 + [VMEM] * 2,
        out_specs=[ANY] * 7,
        scratch_shapes=[
            pltpu.VMEM((D, 3 * GROUP), BF16),
            pltpu.VMEM((4, TOKENS, D), BF16),
            pltpu.VMEM((4, TOKENS, GROUP), BF16),
            pltpu.VMEM((4, TOKENS, 2 * GROUP), BF16),
            pltpu.SemaphoreType.DMA((16,)),
            pltpu.SemaphoreType.DMA((5,)),
            pltpu.SemaphoreType.DMA((4, 4)),
        ],
        compiler_params=PARAMS,
        cost_estimate=LIGHT,
    )(place, *tokens, *pieces, query_gain.reshape(1, HD), key_gain.reshape(1, HD))


def fold(scores):
    return jnp.maximum(scores[:, :HD], scores[:, HD:])


def attend_tiles(query, groups, peak, total):
    ones = jnp.ones((TOKENS, HD), BF16)
    scored = []
    best = peak
    for cost, tiles in groups:
        top = None
        for tile in tiles:
            scores = lax.dot_general(
                query, tile[:, :HD], (((1,), (1,)), ((), ())), preferred_element_type=F32
            )
            scored.append((cost, scores))
            folded = fold(scores)
            top = folded if top is None else jnp.maximum(top, folded)
        top = top * SCORE_SCALE
        if cost is not None:
            top = top - cost
        best = top if best is None else jnp.maximum(best, top)
    high = jnp.max(best, axis=1, keepdims=True)
    weights = []
    for cost, scores in scored:
        base = high if cost is None else high + cost
        weights.append(jnp.exp2(scores * SCORE_SCALE - base).astype(BF16))
    wide = [jnp.concatenate([tile[:, HD:], ones], axis=1) for _, tiles in groups for tile in tiles]
    mixed = jnp.dot(
        jnp.concatenate(weights, axis=1), jnp.concatenate(wide, axis=0), preferred_element_type=F32
    )
    if total is not None:
        scale = jnp.exp2(peak - high)
        mixed = mixed + total * jnp.concatenate([scale, scale], axis=1)
    return high, mixed


def penalty(flag):
    return jnp.where(flag > 0, 0.0, 1e30).astype(F32)


def near_kernel(q, own, mate, *states):
    peaks, totals = states[:2], states[2:]
    for yl in range(2):
        for role in range(2):
            tiles = [own[role, 0], own[role, 1], mate[1, 0], mate[1, 1]]
            if role:
                tiles += [mate[0, 0], mate[0, 1]]
            peak, total = attend_tiles(q[role * 2 + yl], [(None, tiles)], None, None)
            peaks[role][0, yl] = jnp.broadcast_to(peak, (TOKENS, HD))
            totals[role][0, yl] = total


def far_kernel(valid, q, *refs):
    peaks, totals = refs[:2], refs[2:4]
    outer_rows, inner_rows, mate_outer_rows, mate_inner_rows, corners = (refs[n : n + 2] for n in range(4, 14, 2))
    edge, outs, done = refs[14], refs[15:19], refs[19]
    core = valid[3]
    for yl in range(2):
        no_row = penalty(valid[yl])
        for role in range(2):
            if role == 0:
                groups = [
                    (no_row, [outer_rows[yl][...], mate_inner_rows[yl][...]]),
                    (penalty(valid[2]), [edge[0], edge[1]]),
                    (jnp.maximum(no_row, penalty(valid[2])), [corners[yl][...]]),
                ]
            else:
                groups = [(no_row, [rows[yl][...] for rows in (inner_rows, mate_inner_rows, mate_outer_rows)])]
            _, total = attend_tiles(q[role * 2 + yl], groups, peaks[role][0, yl], totals[role][0, yl])
            yh = 1 - core if role else core
            done[yh * 2 + yl] = (total[:, :HD] / total[:, HD:]).astype(BF16)
    for out, step in zip(outs, STEPS, strict=True):
        out[...] = done[lax.rem(valid[4] - step + 4, 4)]


def penalty(flag):
    return jnp.where(flag > 0, 0.0, 1e30).astype(F32)


def head_spec(array, width):
    lead = array.ndim - 1
    return pl.BlockSpec(array.shape[:-1] + (width,), lambda h: (0,) * lead + (h,))


PEAK, TOTAL = (
    (
        jax.ShapeDtypeStruct((GROUP_HEADS, 2, TOKENS, width), F32),
        pl.BlockSpec((1, 2, TOKENS, width), lambda h: (h, 0, 0, 0)),
    )
    for width in (HD, 2 * HD)
)


def attend_near(q, own, mate):
    return pl.pallas_call(
        near_kernel,
        name="attend_near",
        grid=(GROUP_HEADS,),
        out_shape=(PEAK[0], PEAK[0], TOTAL[0], TOTAL[0]),
        in_specs=[head_spec(q, HD), head_spec(own, 2 * HD), head_spec(mate, 2 * HD)],
        out_specs=[PEAK[1], PEAK[1], TOTAL[1], TOTAL[1]],
        compiler_params=NEAR,
        cost_estimate=LIGHT,
    )(q, own, mate)


def attend_far(valid, q, peaks, totals, *kv):
    return pl.pallas_call(
        far_kernel,
        name="attend_far",
        grid=(GROUP_HEADS,),
        out_shape=(jax.ShapeDtypeStruct((TOKENS, GROUP), BF16),) * 4,
        in_specs=[SMEM, head_spec(q, HD), PEAK[1], PEAK[1], TOTAL[1], TOTAL[1]]
        + [head_spec(a, 2 * HD) for a in kv],
        out_specs=[pl.BlockSpec((TOKENS, HD), lambda h: (0, h))] * 4,
        scratch_shapes=[pltpu.VMEM((4, TOKENS, HD), BF16)],
        compiler_params=FAR,
        cost_estimate=LIGHT,
    )(valid, q, *peaks, *totals, *kv)


def side_kernel(place, *refs):
    for part, step in zip(refs[:4], STEPS, strict=True):
        start = lax.rem(place[0] + step + 4, 4) * GROUP
        refs[4][:, pl.ds(pl.multiple_of(start, HD), GROUP)] = part[...]


def side_by_side(place, parts, shape):
    return pl.pallas_call(
        side_kernel,
        name="side_by_side",
        out_shape=jax.ShapeDtypeStruct((TOKENS, D), BF16),
        in_specs=[SMEM] + [VMEM] * 4,
        out_specs=VMEM,
        compiler_params=SIDE,
    )(place, *parts).reshape(shape)


def per_device(hidden, projection, adaptive_shift, adaptive_scale, query_gain, key_gain):
    z, yl, x, yh, core = (lax.axis_index(a) for a in AXES)
    y = yh * 2 + yl
    inner = projection.shape[1] // 3

    def columns(chip, *kinds):
        parts = [lax.dynamic_slice_in_dim(projection, k * inner + chip * GROUP, GROUP, 1) for k in kinds]
        return parts[0] if len(parts) == 1 else jnp.concatenate(parts, axis=1)

    normed = layer_norm(hidden.reshape(TOKENS, D), adaptive_shift, adaptive_scale)
    theirs = swap_rows(columns(yh * 2 + 1 - yl, 1, 2, 0))
    normed = after(normed, theirs)
    behind, ahead = shift(normed, dy=1), shift(normed, dy=-1)
    base = jnp.concatenate([columns(y, 1, 2, 0), theirs], axis=0)
    base = after(base, normed)
    ring = [base, ring_step(base)]
    ring.append(ring_step(ring[1]))
    ring.append(ring_step(after(ring[2], behind, ahead)))
    ring.append(ring_step(ring[3]))
    opposite = [shift(behind[:HALF], dy=1), shift(ahead[HALF:], dy=-1)]
    pieces = ring + [swap_cores(ring[1]), swap_cores(ring[2]), swap_cores(after(ring[3], *opposite))]
    tokens = [normed, behind, ahead] + opposite

    place = jnp.stack([y, core, z]).astype(jnp.int32)
    q, own, edge_out, outer_low, outer_high, inner_low, inner_high = project(
        place, tokens, pieces, query_gain, key_gain
    )
    outer_below = shift(outer_high, dz=1)
    outer_above = shift(outer_low, dz=-1)
    edge = outward(edge_out)
    mate = swap_cores(own)
    inner_below = shift(after(inner_high, mate), dz=1)
    inner_above = shift(after(inner_low, mate), dz=-1)
    outer_peak, inner_peak, outer_total, inner_total = attend_near(q, own, mate)
    corner_below = outward(after(outer_below, inner_peak))
    corner_above = outward(after(outer_above, inner_peak))
    last_x = jnp.where(core == 0, 0, 3)
    valid = jnp.stack([z > 0, z < 7, x != last_x, core, y]).astype(jnp.int32)
    outer_rows, inner_rows = (outer_below, outer_above), (inner_below, inner_above)
    mate_outer_rows = [swap_cores(after(row, *inner_rows)) for row in outer_rows]
    mate_inner_rows = [swap_cores(after(row, inner_peak)) for row in inner_rows]
    attended = attend_far(
        valid,
        q,
        (outer_peak, inner_peak),
        (outer_total, inner_total),
        *outer_rows,
        *inner_rows,
        *mate_outer_rows,
        *mate_inner_rows,
        corner_below,
        corner_above,
        edge,
    )
    back = [attended[0]] + [shift(tile, dy=-step) for step, tile in zip(STEPS[1:], attended[1:], strict=True)]
    return side_by_side(place, back, hidden.shape)


def solution(mesh):
    split = Mesh(np.asarray(mesh.devices).reshape(SIZES), AXES)
    tm, height = ("z", "yl"), ("x", "yh", "core")
    return jax.shard_map(
        per_device,
        mesh=split,
        in_specs=(P(tm, height, None, None), P(tm, None), P(), P(), P(), P()),
        out_specs=P(tm, height, None, None),
        check_vma=False,
    )
```

```python
import math

import jax
import jax.numpy as jnp
import numpy as np
from jax import lax
from jax.experimental import pallas as pl
from jax.experimental.pallas import tpu as pltpu
from jax.sharding import Mesh, PartitionSpec as P

AXES = ("z", "yl", "x", "yh", "core")
SIZES = (8, 2, 4, 2, 2)
TOKENS = 256
D = 1536
HD = 128
GROUP_HEADS = 3
GROUP = GROUP_HEADS * HD
ROWS = 96
EPSILON = 1e-06
SCORE_SCALE = HD ** (-0.5) * math.log2(math.e)
F32 = jnp.float32
BF16 = jnp.bfloat16


def linear(z, y, x, core):
    return (((z % 8 * 2 + y % 2) * 4 + x % 4) * 2 + y % 4 // 2) * 2 + core


def pairs(move):
    return [
        (linear(z, y, x, core), linear(*move(z, y, x, core)))
        for z in range(8)
        for y in range(4)
        for x in range(4)
        for core in range(2)
    ]


def shift(array, dz=0, dy=0):
    return lax.ppermute(array, AXES, pairs(lambda z, y, x, core: (z + dz, y + dy, x, core)))


def swap_cores(array):
    return lax.ppermute(array, AXES, pairs(lambda z, y, x, core: (z, y, x, 1 - core)))


def outward(array, dz=0):
    return lax.ppermute(
        array, AXES, pairs(lambda z, y, x, core: (z + dz, y, x + (1 if core else -1), 1 - core))
    )


def ring_step(array):
    return lax.ppermute(
        array, AXES, pairs(lambda z, y, x, core: (z + (-1 if core else 1), y, x, core))
    )


def swap_rows(array):
    return lax.ppermute(
        array, AXES, pairs(lambda z, y, x, core: (z, y // 2 * 2 + 1 - y % 2, x, core))
    )


def after(array, *others):
    return lax.optimization_barrier((array,) + others)[0]


def layer_norm(activations, adaptive_shift, adaptive_scale):
    centre = jnp.mean(activations, axis=1, keepdims=True)
    shifted = activations - centre
    spread = jnp.mean(shifted * shifted, axis=1, keepdims=True)
    scaled = shifted * lax.rsqrt(spread + EPSILON) * (1.0 + adaptive_scale) + adaptive_shift
    return scaled.astype(BF16)


STEPS = (0, 1, -1, 2)
HALF = TOKENS // 2
VMEM = pl.BlockSpec(memory_space=pltpu.VMEM)
SMEM = pl.BlockSpec(memory_space=pltpu.SMEM)
PARAMS = pltpu.CompilerParams(vmem_limit_bytes=60 * 1024 * 1024)
NEAR = pltpu.CompilerParams(vmem_limit_bytes=60 * 1024 * 1024)
FAR = pltpu.CompilerParams(vmem_limit_bytes=60 * 1024 * 1024)
SIDE = pltpu.CompilerParams(vmem_limit_bytes=8 * 1024 * 1024)


def weight_copies(weights, pieces, sems, z, yl, core):
    sign = 2 * core - 1
    offsets = [0] + [sign * r for r in range(1, 5)] + [-sign * r for r in range(1, 4)]
    copies = []
    for index, (piece, offset) in enumerate(zip(pieces, offsets, strict=True)):
        start = lax.rem(z + offset + 8, 8) * (2 * ROWS)
        for half, lo in ((0, yl), (1, 1 - yl)):
            where = pl.ds(pl.multiple_of(start + lo * ROWS, 32), ROWS)
            copies.append(
                pltpu.make_async_copy(
                    piece.at[pl.ds(half * ROWS, ROWS)], weights.at[where], sems.at[2 * index + half]
                )
            )
    return copies


def head_norm(block, gain):
    mean_square = jnp.mean(block * block, axis=1, keepdims=True)
    return (block * lax.rsqrt(mean_square + EPSILON) * gain[...]).astype(BF16)


def sources(y, core):
    found = []
    for step in STEPS:
        source = lax.rem(y - step + 4, 4)
        found.append((lax.rem(source, 2), jnp.where(source // 2 == core, 0, 1)))
    return found


def token_copies(rows, tokens, slots, sems):
    copies = [pltpu.make_async_copy(tokens[n], rows.at[slots[n]], sems.at[n]) for n in range(3)]
    for half in range(2):
        where = rows.at[slots[3], pl.ds(half * HALF, HALF)]
        copies.append(pltpu.make_async_copy(tokens[3 + half], where, sems.at[3 + half]))
    return copies


def project_kernel(place, *refs):
    tokens, pieces = refs[:5], refs[5:13]
    query_gain, key_gain, q_out, own, edge = refs[13:18]
    alone = refs[18:22]
    weights, rows, q_done, kv_done, sems, token_sems, out_sems = refs[22:]
    y, core = place[0], place[1]
    slots = [role * 2 + yl for yl, role in sources(y, core)]
    copies = weight_copies(weights, pieces, sems, place[2], lax.rem(y, 2), core)
    copies += token_copies(rows, tokens, slots, token_sems)
    for copy in copies:
        copy.start()
    for copy in copies:
        copy.wait()
    leaving = []
    for slot in range(4):
        role, yl = slot // 2, slot % 2
        projected = jnp.dot(rows[slot], weights[...], preferred_element_type=F32)
        for head in range(GROUP_HEADS):
            ks = slice(head * 2 * HD, head * 2 * HD + HD)
            vs = slice(head * 2 * HD + HD, (head + 1) * 2 * HD)
            span = slice(head * HD, (head + 1) * HD)
            part = lambda kind: projected[:, kind * GROUP + head * HD : kind * GROUP + (head + 1) * HD]
            kv_done[slot, :, ks] = head_norm(part(0), key_gain)
            kv_done[slot, :, vs] = part(1).astype(BF16)
            q_done[slot, :, span] = head_norm(part(2), query_gain)
        targets = [own.at[role, yl], alone[slot]] + ([edge.at[yl]] if role == 0 else [])
        moves = [(kv_done.at[slot], target) for target in targets] + [(q_done.at[slot], q_out.at[slot])]
        for index, (source, target) in enumerate(moves):
            leaving.append(pltpu.make_async_copy(source, target, out_sems.at[slot, index]))
            leaving[-1].start()
    for copy in leaving:
        copy.wait()


ANY = pl.BlockSpec(memory_space=pl.ANY)
LIGHT = pl.CostEstimate(flops=10_000_000, bytes_accessed=100_000, transcendentals=0)


def project(place, tokens, pieces, query_gain, key_gain):
    kv = lambda *lead: jax.ShapeDtypeStruct(lead + (TOKENS, 2 * GROUP), BF16)
    return pl.pallas_call(
        project_kernel,
        name="project",
        out_shape=(jax.ShapeDtypeStruct((4, TOKENS, GROUP), BF16), kv(2, 2), kv(2)) + (kv(),) * 4,
        in_specs=[SMEM] + [ANY] * 13 + [VMEM] * 2,
        out_specs=[ANY] * 7,
        scratch_shapes=[
            pltpu.VMEM((D, 3 * GROUP), BF16),
            pltpu.VMEM((4, TOKENS, D), BF16),
            pltpu.VMEM((4, TOKENS, GROUP), BF16),
            pltpu.VMEM((4, TOKENS, 2 * GROUP), BF16),
            pltpu.SemaphoreType.DMA((16,)),
            pltpu.SemaphoreType.DMA((5,)),
            pltpu.SemaphoreType.DMA((4, 4)),
        ],
        compiler_params=PARAMS,
        cost_estimate=LIGHT,
    )(place, *tokens, *pieces, query_gain.reshape(1, HD), key_gain.reshape(1, HD))


def fold(scores):
    return jnp.maximum(scores[:, :HD], scores[:, HD:])


def attend_tiles(query, groups, peak, total):
    ones = jnp.ones((TOKENS, HD), BF16)
    scored = []
    best = peak
    for cost, tiles in groups:
        top = None
        for tile in tiles:
            scores = lax.dot_general(
                query, tile[:, :HD], (((1,), (1,)), ((), ())), preferred_element_type=F32
            )
            scored.append((cost, scores))
            folded = fold(scores)
            top = folded if top is None else jnp.maximum(top, folded)
        top = top * SCORE_SCALE
        if cost is not None:
            top = top - cost
        best = top if best is None else jnp.maximum(best, top)
    high = jnp.max(best, axis=1, keepdims=True)
    weights = []
    for cost, scores in scored:
        base = high if cost is None else high + cost
        weights.append(jnp.exp2(scores * SCORE_SCALE - base).astype(BF16))
    wide = [jnp.concatenate([tile[:, HD:], ones], axis=1) for _, tiles in groups for tile in tiles]
    mixed = jnp.dot(
        jnp.concatenate(weights, axis=1), jnp.concatenate(wide, axis=0), preferred_element_type=F32
    )
    if total is not None:
        scale = jnp.exp2(peak - high)
        mixed = mixed + total * jnp.concatenate([scale, scale], axis=1)
    return high, mixed


def penalty(flag):
    return jnp.where(flag > 0, 0.0, 1e30).astype(F32)


def near_kernel(q, own, mate, *states):
    peaks, totals = states[:2], states[2:]
    for yl in range(2):
        for role in range(2):
            tiles = [own[role, 0], own[role, 1], mate[1, 0], mate[1, 1]]
            if role:
                tiles += [mate[0, 0], mate[0, 1]]
            peak, total = attend_tiles(q[role * 2 + yl], [(None, tiles)], None, None)
            peaks[role][0, yl] = jnp.broadcast_to(peak, (TOKENS, HD))
            totals[role][0, yl] = total


def far_kernel(valid, q, *refs):
    peaks, totals = refs[:2], refs[2:4]
    outer_rows, inner_rows, mate_outer_rows, mate_inner_rows, corners = (refs[n : n + 2] for n in range(4, 14, 2))
    edge, outs, done = refs[14], refs[15:19], refs[19]
    core = valid[3]
    for yl in range(2):
        no_row = penalty(valid[yl])
        for role in range(2):
            if role == 0:
                groups = [
                    (no_row, [outer_rows[yl][...], mate_inner_rows[yl][...]]),
                    (penalty(valid[2]), [edge[0], edge[1]]),
                    (jnp.maximum(no_row, penalty(valid[2])), [corners[yl][...]]),
                ]
            else:
                groups = [(no_row, [rows[yl][...] for rows in (inner_rows, mate_inner_rows, mate_outer_rows)])]
            _, total = attend_tiles(q[role * 2 + yl], groups, peaks[role][0, yl], totals[role][0, yl])
            yh = 1 - core if role else core
            done[yh * 2 + yl] = (total[:, :HD] / total[:, HD:]).astype(BF16)
    for out, step in zip(outs, STEPS, strict=True):
        out[...] = done[lax.rem(valid[4] - step + 4, 4)]


def penalty(flag):
    return jnp.where(flag > 0, 0.0, 1e30).astype(F32)


def head_spec(array, width):
    lead = array.ndim - 1
    return pl.BlockSpec(array.shape[:-1] + (width,), lambda h, *_: (0,) * lead + (h,))


PEAK, TOTAL = (
    (
        jax.ShapeDtypeStruct((GROUP_HEADS, 2, TOKENS, width), F32),
        pl.BlockSpec((1, 2, TOKENS, width), lambda h, *_: (h, 0, 0, 0)),
    )
    for width in (HD, 2 * HD)
)


def attend_near(q, own, mate):
    return pl.pallas_call(
        near_kernel,
        name="attend_near",
        grid=(GROUP_HEADS,),
        out_shape=(PEAK[0], PEAK[0], TOTAL[0], TOTAL[0]),
        in_specs=[head_spec(q, HD), head_spec(own, 2 * HD), head_spec(mate, 2 * HD)],
        out_specs=[PEAK[1], PEAK[1], TOTAL[1], TOTAL[1]],
        compiler_params=NEAR,
        cost_estimate=LIGHT,
    )(q, own, mate)


def attend_far(valid, q, peaks, totals, *kv):
    part = jax.ShapeDtypeStruct((TOKENS, GROUP), BF16)
    part_spec = pl.BlockSpec((TOKENS, HD), lambda h, info: (0, h))
    return pl.pallas_call(
        far_kernel,
        name="attend_far",
        grid_spec=pltpu.PrefetchScalarGridSpec(
            num_scalar_prefetch=1,
            grid=(GROUP_HEADS,),
            in_specs=[head_spec(q, HD), PEAK[1], PEAK[1], TOTAL[1], TOTAL[1]]
            + [head_spec(a, 2 * HD) for a in kv],
            out_specs=[pl.BlockSpec((TOKENS, HD), lambda h, info: (0, info[4] * GROUP_HEADS + h))]
            + [part_spec] * 3,
            scratch_shapes=[pltpu.VMEM((4, TOKENS, HD), BF16)],
        ),
        out_shape=(jax.ShapeDtypeStruct((TOKENS, D), BF16), part, part, part),
        compiler_params=FAR,
        cost_estimate=LIGHT,
    )(valid, q, *peaks, *totals, *kv)


def side_kernel(place, *refs):
    parts, out, sems = refs[:3], refs[4], refs[5]
    copies = []
    for n, (part, step) in enumerate(zip(parts, STEPS[1:], strict=True)):
        start = lax.rem(place[0] + step + 4, 4) * GROUP
        where = out.at[:, pl.ds(pl.multiple_of(start, HD), GROUP)]
        copies.append(pltpu.make_async_copy(part, where, sems.at[n]))
    for copy in copies:
        copy.start()
    for copy in copies:
        copy.wait()


def side_by_side(place, whole, parts, shape):
    return pl.pallas_call(
        side_kernel,
        name="side_by_side",
        out_shape=jax.ShapeDtypeStruct((TOKENS, D), BF16),
        in_specs=[SMEM] + [VMEM] * 3 + [ANY],
        out_specs=ANY,
        scratch_shapes=[pltpu.SemaphoreType.DMA((3,))],
        input_output_aliases={4: 0},
        compiler_params=SIDE,
        cost_estimate=LIGHT,
    )(place, *parts, whole).reshape(shape)


def per_device(hidden, projection, adaptive_shift, adaptive_scale, query_gain, key_gain):
    z, yl, x, yh, core = (lax.axis_index(a) for a in AXES)
    y = yh * 2 + yl
    inner = projection.shape[1] // 3

    def columns(chip, *kinds):
        parts = [lax.dynamic_slice_in_dim(projection, k * inner + chip * GROUP, GROUP, 1) for k in kinds]
        return parts[0] if len(parts) == 1 else jnp.concatenate(parts, axis=1)

    normed = layer_norm(hidden.reshape(TOKENS, D), adaptive_shift, adaptive_scale)
    theirs = swap_rows(columns(yh * 2 + 1 - yl, 1, 2, 0))
    normed = after(normed, theirs)
    behind, ahead = shift(normed, dy=1), shift(normed, dy=-1)
    base = jnp.concatenate([columns(y, 1, 2, 0), theirs], axis=0)
    base = after(base, normed)
    ring = [base, ring_step(base)]
    ring.append(ring_step(ring[1]))
    ring.append(ring_step(after(ring[2], behind, ahead)))
    ring.append(ring_step(ring[3]))
    opposite = [shift(behind[:HALF], dy=1), shift(ahead[HALF:], dy=-1)]
    pieces = ring + [swap_cores(ring[1]), swap_cores(ring[2]), swap_cores(after(ring[3], *opposite))]
    tokens = [normed, behind, ahead] + opposite

    place = jnp.stack([y, core, z]).astype(jnp.int32)
    q, own, edge_out, outer_low, outer_high, inner_low, inner_high = project(
        place, tokens, pieces, query_gain, key_gain
    )
    outer_below = shift(outer_high, dz=1)
    outer_above = shift(outer_low, dz=-1)
    edge = outward(edge_out)
    mate = swap_cores(own)
    inner_below = shift(after(inner_high, mate), dz=1)
    inner_above = shift(after(inner_low, mate), dz=-1)
    outer_peak, inner_peak, outer_total, inner_total = attend_near(q, own, mate)
    corner_below = outward(after(outer_below, inner_peak))
    corner_above = outward(after(outer_above, inner_peak))
    last_x = jnp.where(core == 0, 0, 3)
    valid = jnp.stack([z > 0, z < 7, x != last_x, core, y]).astype(jnp.int32)
    outer_rows, inner_rows = (outer_below, outer_above), (inner_below, inner_above)
    mate_outer_rows = [swap_cores(after(row, *inner_rows)) for row in outer_rows]
    mate_inner_rows = [swap_cores(after(row, inner_peak)) for row in inner_rows]
    attended = attend_far(
        valid,
        q,
        (outer_peak, inner_peak),
        (outer_total, inner_total),
        *outer_rows,
        *inner_rows,
        *mate_outer_rows,
        *mate_inner_rows,
        corner_below,
        corner_above,
        edge,
    )
    back = [shift(tile, dy=-step) for step, tile in zip(STEPS[1:], attended[1:], strict=True)]
    return side_by_side(place, attended[0], back, hidden.shape)


def solution(mesh):
    split = Mesh(np.asarray(mesh.devices).reshape(SIZES), AXES)
    tm, height = ("z", "yl"), ("x", "yh", "core")
    return jax.shard_map(
        per_device,
        mesh=split,
        in_specs=(P(tm, height, None, None), P(tm, None), P(), P(), P(), P()),
        out_specs=P(tm, height, None, None),
        check_vma=False,
    )
```

```python
import math

import jax
import jax.numpy as jnp
import numpy as np
from jax import lax
from jax.experimental import pallas as pl
from jax.experimental.pallas import tpu as pltpu
from jax.sharding import Mesh, PartitionSpec as P

AXES = ("z", "yl", "x", "yh", "core")
SIZES = (8, 2, 4, 2, 2)
TOKENS = 256
D = 1536
HD = 128
GROUP_HEADS = 3
GROUP = GROUP_HEADS * HD
ROWS = 96
EPSILON = 1e-06
SCORE_SCALE = HD ** (-0.5) * math.log2(math.e)
F32 = jnp.float32
BF16 = jnp.bfloat16


def linear(z, y, x, core):
    return (((z % 8 * 2 + y % 2) * 4 + x % 4) * 2 + y % 4 // 2) * 2 + core


def pairs(move):
    return [
        (linear(z, y, x, core), linear(*move(z, y, x, core)))
        for z in range(8)
        for y in range(4)
        for x in range(4)
        for core in range(2)
    ]


def shift(array, dz=0, dy=0):
    return lax.ppermute(array, AXES, pairs(lambda z, y, x, core: (z + dz, y + dy, x, core)))


def swap_cores(array):
    return lax.ppermute(array, AXES, pairs(lambda z, y, x, core: (z, y, x, 1 - core)))


def outward(array, dz=0):
    return lax.ppermute(
        array, AXES, pairs(lambda z, y, x, core: (z + dz, y, x + (1 if core else -1), 1 - core))
    )


def ring_step(array):
    return lax.ppermute(
        array, AXES, pairs(lambda z, y, x, core: (z + (-1 if core else 1), y, x, core))
    )


def swap_rows(array):
    return lax.ppermute(
        array, AXES, pairs(lambda z, y, x, core: (z, y // 2 * 2 + 1 - y % 2, x, core))
    )


def after(array, *others):
    return lax.optimization_barrier((array,) + others)[0]


def layer_norm(activations, adaptive_shift, adaptive_scale):
    centre = jnp.mean(activations, axis=1, keepdims=True)
    shifted = activations - centre
    spread = jnp.mean(shifted * shifted, axis=1, keepdims=True)
    scaled = shifted * lax.rsqrt(spread + EPSILON) * (1.0 + adaptive_scale) + adaptive_shift
    return scaled.astype(BF16)


STEPS = (0, 1, -1, 2)
HALF = TOKENS // 2
VMEM = pl.BlockSpec(memory_space=pltpu.VMEM)
SMEM = pl.BlockSpec(memory_space=pltpu.SMEM)
PARAMS = pltpu.CompilerParams(vmem_limit_bytes=60 * 1024 * 1024)
NEAR = pltpu.CompilerParams(vmem_limit_bytes=60 * 1024 * 1024)
FAR = pltpu.CompilerParams(vmem_limit_bytes=60 * 1024 * 1024)
SIDE = pltpu.CompilerParams(vmem_limit_bytes=8 * 1024 * 1024)


def weight_copies(weights, pieces, sems, z, yl, core):
    sign = 2 * core - 1
    offsets = [0] + [sign * r for r in range(1, 5)] + [-sign * r for r in range(1, 4)]
    copies = []
    for index, (piece, offset) in enumerate(zip(pieces, offsets, strict=True)):
        start = lax.rem(z + offset + 8, 8) * (2 * ROWS)
        for half, lo in ((0, yl), (1, 1 - yl)):
            where = pl.ds(pl.multiple_of(start + lo * ROWS, 32), ROWS)
            copies.append(
                pltpu.make_async_copy(
                    piece.at[pl.ds(half * ROWS, ROWS)], weights.at[where], sems.at[2 * index + half]
                )
            )
    return copies


def head_norm(block, gain):
    mean_square = jnp.mean(block * block, axis=1, keepdims=True)
    return (block * lax.rsqrt(mean_square + EPSILON) * gain[...]).astype(BF16)


def sources(y, core):
    found = []
    for step in STEPS:
        source = lax.rem(y - step + 4, 4)
        found.append((lax.rem(source, 2), jnp.where(source // 2 == core, 0, 1)))
    return found


def token_copies(rows, tokens, slots, sems):
    copies = [pltpu.make_async_copy(tokens[n], rows.at[slots[n]], sems.at[n]) for n in range(3)]
    for half in range(2):
        where = rows.at[slots[3], pl.ds(half * HALF, HALF)]
        copies.append(pltpu.make_async_copy(tokens[3 + half], where, sems.at[3 + half]))
    return copies


def project_kernel(place, *refs):
    tokens, pieces = refs[:5], refs[5:13]
    query_gain, key_gain, q_out, own, edge = refs[13:18]
    alone = refs[18:22]
    weights, rows, q_done, kv_done, sems, token_sems, out_sems = refs[22:]
    y, core = place[0], place[1]
    slots = [role * 2 + yl for yl, role in sources(y, core)]
    copies = weight_copies(weights, pieces, sems, place[2], lax.rem(y, 2), core)
    copies += token_copies(rows, tokens, slots, token_sems)
    for copy in copies:
        copy.start()
    for copy in copies:
        copy.wait()
    leaving = []
    for slot in range(4):
        role, yl = slot // 2, slot % 2
        projected = jnp.dot(rows[slot], weights[...], preferred_element_type=F32)
        for head in range(GROUP_HEADS):
            ks = slice(head * 2 * HD, head * 2 * HD + HD)
            vs = slice(head * 2 * HD + HD, (head + 1) * 2 * HD)
            span = slice(head * HD, (head + 1) * HD)
            part = lambda kind: projected[:, kind * GROUP + head * HD : kind * GROUP + (head + 1) * HD]
            kv_done[slot, :, ks] = head_norm(part(0), key_gain)
            kv_done[slot, :, vs] = part(1).astype(BF16)
            q_done[slot, :, span] = head_norm(part(2), query_gain)
        targets = [own.at[role, yl], alone[slot]] + ([edge.at[yl]] if role == 0 else [])
        moves = [(kv_done.at[slot], target) for target in targets] + [(q_done.at[slot], q_out.at[slot])]
        for index, (source, target) in enumerate(moves):
            leaving.append(pltpu.make_async_copy(source, target, out_sems.at[slot, index]))
            leaving[-1].start()
    for copy in leaving:
        copy.wait()


ANY = pl.BlockSpec(memory_space=pl.ANY)
LIGHT = pl.CostEstimate(flops=10_000_000, bytes_accessed=100_000, transcendentals=0)


def project(place, tokens, pieces, query_gain, key_gain):
    kv = lambda *lead: jax.ShapeDtypeStruct(lead + (TOKENS, 2 * GROUP), BF16)
    return pl.pallas_call(
        project_kernel,
        name="project",
        out_shape=(jax.ShapeDtypeStruct((4, TOKENS, GROUP), BF16), kv(2, 2), kv(2)) + (kv(),) * 4,
        in_specs=[SMEM] + [ANY] * 13 + [VMEM] * 2,
        out_specs=[ANY] * 7,
        scratch_shapes=[
            pltpu.VMEM((D, 3 * GROUP), BF16),
            pltpu.VMEM((4, TOKENS, D), BF16),
            pltpu.VMEM((4, TOKENS, GROUP), BF16),
            pltpu.VMEM((4, TOKENS, 2 * GROUP), BF16),
            pltpu.SemaphoreType.DMA((16,)),
            pltpu.SemaphoreType.DMA((5,)),
            pltpu.SemaphoreType.DMA((4, 4)),
        ],
        compiler_params=PARAMS,
        cost_estimate=LIGHT,
    )(place, *tokens, *pieces, query_gain.reshape(1, HD), key_gain.reshape(1, HD))


def fold(scores):
    return jnp.maximum(scores[:, :HD], scores[:, HD:])


def attend_tiles(query, groups, peak, total):
    ones = jnp.ones((TOKENS, HD), BF16)
    scored = []
    best = peak
    for cost, tiles in groups:
        top = None
        for tile in tiles:
            scores = lax.dot_general(
                query, tile[:, :HD], (((1,), (1,)), ((), ())), preferred_element_type=F32
            )
            scored.append((cost, scores))
            folded = fold(scores)
            top = folded if top is None else jnp.maximum(top, folded)
        top = top * SCORE_SCALE
        if cost is not None:
            top = top - cost
        best = top if best is None else jnp.maximum(best, top)
    high = jnp.max(best, axis=1, keepdims=True)
    weights = []
    for cost, scores in scored:
        base = high if cost is None else high + cost
        weights.append(jnp.exp2(scores * SCORE_SCALE - base).astype(BF16))
    wide = [jnp.concatenate([tile[:, HD:], ones], axis=1) for _, tiles in groups for tile in tiles]
    mixed = jnp.dot(
        jnp.concatenate(weights, axis=1), jnp.concatenate(wide, axis=0), preferred_element_type=F32
    )
    if total is not None:
        scale = jnp.exp2(peak - high)
        mixed = mixed + total * jnp.concatenate([scale, scale], axis=1)
    return high, mixed


def penalty(flag):
    return jnp.where(flag > 0, 0.0, 1e30).astype(F32)


def near_kernel(q, own, mate, *states):
    peaks, totals = states[:2], states[2:]
    for yl in range(2):
        for role in range(2):
            tiles = [own[role, 0], own[role, 1], mate[1, 0], mate[1, 1]]
            if role:
                tiles += [mate[0, 0], mate[0, 1]]
            peak, total = attend_tiles(q[role * 2 + yl], [(None, tiles)], None, None)
            peaks[role][0, yl] = jnp.broadcast_to(peak, (TOKENS, HD))
            totals[role][0, yl] = total


def far_kernel(valid, q, *refs):
    peaks, totals = refs[:2], refs[2:4]
    outer_rows, inner_rows, mate_outer_rows, mate_inner_rows, corners = (refs[n : n + 2] for n in range(4, 14, 2))
    edge, outs, done = refs[14], refs[15:19], refs[19]
    core = valid[3]
    for yl in range(2):
        no_row = penalty(valid[yl])
        for role in range(2):
            if role == 0:
                groups = [
                    (no_row, [outer_rows[yl][...], mate_inner_rows[yl][...]]),
                    (penalty(valid[2]), [edge[0], edge[1]]),
                    (jnp.maximum(no_row, penalty(valid[2])), [corners[yl][...]]),
                ]
            else:
                groups = [(no_row, [rows[yl][...] for rows in (inner_rows, mate_inner_rows, mate_outer_rows)])]
            _, total = attend_tiles(q[role * 2 + yl], groups, peaks[role][0, yl], totals[role][0, yl])
            yh = 1 - core if role else core
            done[yh * 2 + yl] = (total[:, :HD] / total[:, HD:]).astype(BF16)
    for out, step in zip(outs, STEPS, strict=True):
        out[...] = done[lax.rem(valid[4] - step + 4, 4)]


def penalty(flag):
    return jnp.where(flag > 0, 0.0, 1e30).astype(F32)


def head_spec(array, width):
    lead = array.ndim - 1
    return pl.BlockSpec(array.shape[:-1] + (width,), lambda h, *_: (0,) * lead + (h,))


PEAK, TOTAL = (
    (
        jax.ShapeDtypeStruct((GROUP_HEADS, 2, TOKENS, width), F32),
        pl.BlockSpec((1, 2, TOKENS, width), lambda h, *_: (h, 0, 0, 0)),
    )
    for width in (HD, 2 * HD)
)


def attend_near(q, own, mate, states=None):
    first = GROUP_HEADS - 1 if states else 0

    def block(array, width):
        lead = array.ndim - 1
        return pl.BlockSpec(array.shape[:-1] + (width,), lambda h: (0,) * lead + (h + first,))

    def state(pair):
        return pl.BlockSpec(pair[1].block_shape, lambda h: (h + first, 0, 0, 0))

    def kernel(*refs):
        near_kernel(*refs[:3], *refs[-4:])

    shapes = (PEAK[0], PEAK[0], TOTAL[0], TOTAL[0])
    return pl.pallas_call(
        kernel,
        name="attend_near_last" if states else "attend_near",
        grid=(1 if states else GROUP_HEADS - 1,),
        out_shape=shapes,
        in_specs=[block(q, HD), block(own, 2 * HD), block(mate, 2 * HD)] + [ANY] * (4 if states else 0),
        out_specs=[state(PEAK), state(PEAK), state(TOTAL), state(TOTAL)],
        input_output_aliases={3 + n: n for n in range(4)} if states else {},
        compiler_params=NEAR,
        cost_estimate=LIGHT,
    )(q, own, mate, *(states or ()))


def attend_far(valid, q, peaks, totals, *kv):
    part = jax.ShapeDtypeStruct((TOKENS, GROUP), BF16)
    part_spec = pl.BlockSpec((TOKENS, HD), lambda h, info: (0, h))
    return pl.pallas_call(
        far_kernel,
        name="attend_far",
        grid_spec=pltpu.PrefetchScalarGridSpec(
            num_scalar_prefetch=1,
            grid=(GROUP_HEADS,),
            in_specs=[head_spec(q, HD), PEAK[1], PEAK[1], TOTAL[1], TOTAL[1]]
            + [head_spec(a, 2 * HD) for a in kv],
            out_specs=[pl.BlockSpec((TOKENS, HD), lambda h, info: (0, info[4] * GROUP_HEADS + h))]
            + [part_spec] * 3,
            scratch_shapes=[pltpu.VMEM((4, TOKENS, HD), BF16)],
        ),
        out_shape=(jax.ShapeDtypeStruct((TOKENS, D), BF16), part, part, part),
        compiler_params=FAR,
        cost_estimate=LIGHT,
    )(valid, q, *peaks, *totals, *kv)


def side_kernel(place, *refs):
    parts, out, sems = refs[:3], refs[4], refs[5]
    copies = []
    for n, (part, step) in enumerate(zip(parts, STEPS[1:], strict=True)):
        start = lax.rem(place[0] + step + 4, 4) * GROUP
        where = out.at[:, pl.ds(pl.multiple_of(start, HD), GROUP)]
        copies.append(pltpu.make_async_copy(part, where, sems.at[n]))
    for copy in copies:
        copy.start()
    for copy in copies:
        copy.wait()


def side_by_side(place, whole, parts, shape):
    return pl.pallas_call(
        side_kernel,
        name="side_by_side",
        out_shape=jax.ShapeDtypeStruct((TOKENS, D), BF16),
        in_specs=[SMEM] + [VMEM] * 3 + [ANY],
        out_specs=ANY,
        scratch_shapes=[pltpu.SemaphoreType.DMA((3,))],
        input_output_aliases={4: 0},
        compiler_params=SIDE,
        cost_estimate=LIGHT,
    )(place, *parts, whole).reshape(shape)


def per_device(hidden, projection, adaptive_shift, adaptive_scale, query_gain, key_gain):
    z, yl, x, yh, core = (lax.axis_index(a) for a in AXES)
    y = yh * 2 + yl
    inner = projection.shape[1] // 3

    def columns(chip, *kinds):
        parts = [lax.dynamic_slice_in_dim(projection, k * inner + chip * GROUP, GROUP, 1) for k in kinds]
        return parts[0] if len(parts) == 1 else jnp.concatenate(parts, axis=1)

    normed = layer_norm(hidden.reshape(TOKENS, D), adaptive_shift, adaptive_scale)
    theirs = swap_rows(columns(yh * 2 + 1 - yl, 1, 2, 0))
    normed = after(normed, theirs)
    behind, ahead = shift(normed, dy=1), shift(normed, dy=-1)
    base = jnp.concatenate([columns(y, 1, 2, 0), theirs], axis=0)
    base = after(base, normed)
    ring = [base, ring_step(base)]
    ring.append(ring_step(ring[1]))
    ring.append(ring_step(after(ring[2], behind, ahead)))
    ring.append(ring_step(ring[3]))
    opposite = [shift(behind[:HALF], dy=1), shift(ahead[HALF:], dy=-1)]
    pieces = ring + [swap_cores(ring[1]), swap_cores(ring[2]), swap_cores(after(ring[3], *opposite))]
    tokens = [normed, behind, ahead] + opposite

    place = jnp.stack([y, core, z]).astype(jnp.int32)
    q, own, edge_out, outer_low, outer_high, inner_low, inner_high = project(
        place, tokens, pieces, query_gain, key_gain
    )
    outer_below = shift(outer_high, dz=1)
    outer_above = shift(outer_low, dz=-1)
    edge = outward(edge_out)
    mate = swap_cores(own)
    inner_below = shift(after(inner_high, mate), dz=1)
    inner_above = shift(after(inner_low, mate), dz=-1)
    states = attend_near(q, own, mate)
    (outer_below, outer_above), states = lax.optimization_barrier(((outer_below, outer_above), states))
    states = attend_near(q, own, mate, states)
    outer_peak, inner_peak, outer_total, inner_total = states
    corner_below = outward(outer_below)
    corner_above = outward(outer_above)
    last_x = jnp.where(core == 0, 0, 3)
    valid = jnp.stack([z > 0, z < 7, x != last_x, core, y]).astype(jnp.int32)
    outer_rows, inner_rows = (outer_below, outer_above), (inner_below, inner_above)
    mate_outer_rows = [swap_cores(after(row, *inner_rows)) for row in outer_rows]
    mate_inner_rows = [swap_cores(after(row, inner_peak)) for row in inner_rows]
    attended = attend_far(
        valid,
        q,
        (outer_peak, inner_peak),
        (outer_total, inner_total),
        *outer_rows,
        *inner_rows,
        *mate_outer_rows,
        *mate_inner_rows,
        corner_below,
        corner_above,
        edge,
    )
    back = [shift(tile, dy=-step) for step, tile in zip(STEPS[1:], attended[1:], strict=True)]
    return side_by_side(place, attended[0], back, hidden.shape)


def solution(mesh):
    split = Mesh(np.asarray(mesh.devices).reshape(SIZES), AXES)
    tm, height = ("z", "yl"), ("x", "yh", "core")
    return jax.shard_map(
        per_device,
        mesh=split,
        in_specs=(P(tm, height, None, None), P(tm, None), P(), P(), P(), P()),
        out_specs=P(tm, height, None, None),
        check_vma=False,
    )
```
